512 devices in a mesh: section: 4 (over x), dp: 16 (over z), expert: 8 (over y, core).
Axes of the slice: x: 4, y: 4, z: 16, core: 2. Of those that a mesh axis runs over, the one named last changes fastest.
Arguments:
- section_input: bfloat16 [4, 16384, 1024], P('section', ('dp', 'expert')), may hold values from -6 to 6
- saved_input: bfloat16 [4, 16384, 1024], P('section', ('dp', 'expert')), may hold values from -6 to 6
- cotangent: bfloat16 [4, 16384, 1024], P('section', ('dp', 'expert')), may hold values from -6 to 6
- routes_forward: int32 [4, 16384, 8], P('section', ('dp', 'expert')), may hold values from 0 to 63, as said below
- gates_forward: float32 [4, 16384, 8], P('section', ('dp', 'expert')), may hold values from 0.5 to 2
- routes_backward: int32 [4, 16384, 8], P('section', ('dp', 'expert')), may hold values from 0 to 63, as said below
- gates_backward: float32 [4, 16384, 8], P('section', ('dp', 'expert')), may hold values from 0.5 to 2
- gate_weight: bfloat16 [4, 8, 1024, 512], P('section', 'expert', 'dp'), may hold values from -0.1875 to 0.1875
- up_weight: bfloat16 [4, 8, 1024, 512], P('section', 'expert', 'dp'), may hold values from -0.1875 to 0.1875
- down_weight: bfloat16 [4, 8, 512, 1024], P('section', 'expert', 'dp'), may hold values from -0.25 to 0.25
Outputs:
- handed: bfloat16 [4, 16384, 1024], P('section', ('dp', 'expert'))
- grad_back: bfloat16 [4, 16384, 1024], P('section', ('dp', 'expert'))
- grad_gate: float32 [4, 8, 1024, 512], P('section', 'expert', 'dp')
- grad_up: float32 [4, 8, 1024, 512], P('section', 'expert', 'dp')
- grad_down: float32 [4, 8, 512, 1024], P('section', 'expert', 'dp')
The draws below stay inside these ranges and needn't reach their ends.
Inputs may be any that keep to these rules, and one draw needn't show every extreme that they name: `routes_forward`: each token names 8 different experts. In every layer, every block of 128 tokens of one device names each expert below 8 between 1 and 32 times, and in every layer some expert below 8 is named exactly 32 times by every block. `routes_backward`: as routes_forward.
All inputs are finite; a program needn't handle non-finite values.
Results may differ from the reference program's by a relative error of at most 0.017.
Values may be sent and summed in bfloat16 or wider, within the bound.
No kernel may reach another device: no remote copies, remote signals or barrier semaphores. Data moves between devices by JAX's collectives and lax.ppermute only.
A program may use at most 64 MiB of HBM per device.

```python
import math
import jax
import jax.numpy as jnp
from jax import lax

D = 1024
FF = 512
ROUTED = 64
TOPK = 8
TOK_DEV = 128
SECTIONS = 4
WINDOW = 8
TOKENS = 16384
CAP = 32
GRAD_ROWS = 2048
N_DP = 16


def route_table(key):
    blocks_count = TOKENS // TOK_DEV
    key_list = jax.random.split(key, 6)
    hot_expert = jax.random.randint(key_list[0], (SECTIONS, 1, 1), 0, WINDOW)
    share_level = jax.random.randint(key_list[1], (SECTIONS, 1, WINDOW), 1, 5)
    count_limit = jnp.maximum(share_level * CAP // 4, 1)
    counts = jax.random.randint(key_list[2], (SECTIONS, blocks_count, WINDOW), 1, count_limit + 1)
    counts = jnp.where(jnp.arange(WINDOW)[None, None, :] == hot_expert, CAP, counts)
    order_keys = jax.random.randint(key_list[3], (SECTIONS, blocks_count, WINDOW, TOK_DEV), 0, 2 ** 20) * TOK_DEV + jnp.arange(TOK_DEV)
    rank_table = jnp.argsort(jnp.argsort(order_keys, axis=-1), axis=-1)
    chosen = jnp.transpose(rank_table < counts[..., None], (0, 1, 3, 2))
    scores = jax.random.randint(key_list[4], (SECTIONS, blocks_count, TOK_DEV, ROUTED), 0, 2 ** 16) * ROUTED + jnp.arange(ROUTED)
    window_part = jnp.where(chosen, scores[..., :WINDOW] + 2 ** 23, -1)
    scores = jnp.concatenate([window_part, scores[..., WINDOW:]], axis=-1)
    _, picked = lax.top_k(scores, TOPK)
    position_keys = jax.random.randint(key_list[5], (SECTIONS, blocks_count, TOK_DEV, TOPK), 0, 2 ** 16) * TOPK + jnp.arange(TOPK)
    reorder = jnp.argsort(position_keys, axis=-1)
    picked = jnp.take_along_axis(picked, reorder, axis=-1)
    return picked.reshape(SECTIONS, TOKENS, TOPK).astype(jnp.int32)


def draw_routes_forward(key, part):
    return route_table(jax.random.fold_in(key, 11))


def draw_routes_backward(key, part):
    return route_table(jax.random.fold_in(key, 23))


def block_scale(own_key, shape, cuts, low, largest):
    factor_of, own = 1.0, jax.random.fold_in(own_key, 6)
    for dim, blocks in cuts:
        heights = jnp.exp(jax.random.uniform(jax.random.fold_in(own, dim), (blocks,), jnp.float32, low / len(cuts), largest / len(cuts)))
        factor_of = factor_of * jnp.repeat(heights, shape[dim] // blocks).reshape([-1 if axis == dim else 1 for axis in range(len(shape))])
    return factor_of


def normal_values(key, dims, deviation, most, pieces=(), held_as=jnp.bfloat16):
    array = jax.random.normal(key, dims, jnp.float32) * deviation
    if len(pieces) > 0:
        array = block_scale(key, dims, pieces, -0.22, 0.18) * array
    return jnp.clip(array, min=-most, max=most).astype(held_as)


def setup_inputs(seed: int = 0) -> dict:
    streams_of = jax.random.split(jax.random.key(seed), 11)
    section_input = normal_values(streams_of[0], (SECTIONS, TOKENS, D), 1.0, 6.0, ((0, 4), (1, 128)))
    saved_input = normal_values(streams_of[1], (SECTIONS, TOKENS, D), 1.0, 6.0, ((0, 4), (1, 128)))
    cotangent = normal_values(streams_of[2], (SECTIONS, TOKENS, D), 1.0, 6.0, ((0, 4), (1, 128)))
    routes_forward = draw_routes_forward(jax.random.fold_in(streams_of[10], 71), 0)
    gates_forward = jnp.clip(jnp.exp(math.log(2.0) - 1.3862944 * jax.random.uniform(streams_of[4], (SECTIONS, TOKENS, TOPK), jnp.float32) ** block_scale(streams_of[4], (SECTIONS, TOKENS, TOPK), ((0, 4), (1, 128)), -0.2, 0.2)), 0.5, 2.0)
    routes_backward = draw_routes_backward(jax.random.fold_in(streams_of[10], 71), 0)
    gates_backward = jnp.clip(jnp.exp(math.log(2.0) - 1.3862944 * jax.random.uniform(streams_of[6], (SECTIONS, TOKENS, TOPK), jnp.float32) ** block_scale(streams_of[6], (SECTIONS, TOKENS, TOPK), ((0, 4), (1, 128)), -0.2, 0.2)), 0.5, 2.0)
    gate_weight = normal_values(streams_of[7], (SECTIONS, WINDOW, D, FF), D ** -0.5, 0.1875, ((0, 4), (1, 8), (2, 16)))
    up_weight = normal_values(streams_of[8], (SECTIONS, WINDOW, D, FF), D ** -0.5, 0.1875, ((0, 4), (1, 8), (2, 16)))
    down_weight = normal_values(streams_of[9], (SECTIONS, WINDOW, FF, D), FF ** -0.5, 0.25, ((0, 4), (1, 8), (2, 16)))
    return {"section_input": section_input, "saved_input": saved_input, "cotangent": cotangent, "routes_forward": routes_forward, "gates_forward": gates_forward, "routes_backward": routes_backward, "gates_backward": gates_backward, "gate_weight": gate_weight, "up_weight": up_weight, "down_weight": down_weight}


EPSILON = 1e-06

def normalize(values):
    widened = values.astype(jnp.float32)
    factor = lax.rsqrt(lax.optimization_barrier(jnp.mean(widened * widened, axis=-1, keepdims=True)) + EPSILON)
    return (widened * factor, factor)

def slot_table(listed):
    hit_table = (listed[:, :, None] == jnp.arange(WINDOW, dtype=jnp.int32)[None, None, :]).astype(jnp.int32)
    flat_hits = hit_table.reshape(-1, WINDOW)
    before = jnp.cumsum(flat_hits, axis=0).astype(jnp.int32) - flat_hits
    ranked = lax.optimization_barrier(jnp.sum(before * flat_hits, axis=1)).astype(jnp.int32).reshape(listed.shape)
    return jnp.where(listed < WINDOW, listed * CAP + ranked, WINDOW * CAP).astype(jnp.int32)

def slot_owner(slot_ids):
    token_total = slot_ids.shape[0]
    token_index = jnp.repeat(jnp.arange(token_total, dtype=jnp.int32), slot_ids.shape[1])
    owners = jnp.full((WINDOW * CAP + 1,), token_total, jnp.int32).at[slot_ids.reshape(-1)].set(token_index)
    return owners[:WINDOW * CAP]

def slot_gates(slot_ids, gate_vals):
    filled = jnp.zeros((WINDOW * CAP + 1,), jnp.float32).at[slot_ids.reshape(-1)].set(gate_vals.reshape(-1).astype(jnp.float32))
    return filled[:WINDOW * CAP]

def pad_rows(row_table):
    extra = jnp.zeros(row_table.shape[:-2] + (1, row_table.shape[-1]), row_table.dtype)
    return jnp.concatenate([row_table, extra], axis=-2)

def gather_rows(row_table, row_index):
    return jax.vmap(lambda segment, positions: segment[positions])(row_table, row_index)

def expert_forward(row_data, gate_full, up_full, down_full):
    gate_act = jnp.dot(row_data, gate_full, preferred_element_type=jnp.float32)
    up_act = jnp.dot(row_data, up_full, preferred_element_type=jnp.float32)
    hidden = (gate_act * jax.nn.sigmoid(gate_act) * up_act).astype(jnp.bfloat16)
    return jnp.dot(hidden, down_full, preferred_element_type=jnp.float32).astype(jnp.bfloat16)

def expert_backward(row_data, grad_rows, gate_full, up_full, down_full):
    gate_act = jnp.dot(row_data, gate_full, preferred_element_type=jnp.float32)
    up_act = jnp.dot(row_data, up_full, preferred_element_type=jnp.float32)
    sigma = jax.nn.sigmoid(gate_act)
    activated = gate_act * sigma
    hidden = (activated * up_act).astype(jnp.bfloat16)
    contract = (((1,), (1,)), ((), ()))
    grad_hidden = lax.dot_general(grad_rows, down_full, contract, preferred_element_type=jnp.float32)
    grad_gate = (grad_hidden * up_act * sigma * (1.0 + gate_act * (1.0 - sigma))).astype(jnp.bfloat16)
    grad_up = (grad_hidden * activated).astype(jnp.bfloat16)
    grad_input = lax.dot_general(grad_gate, gate_full, contract, preferred_element_type=jnp.float32)
    grad_input = grad_input + lax.dot_general(grad_up, up_full, contract, preferred_element_type=jnp.float32)
    return (hidden, grad_gate, grad_up, grad_input.astype(jnp.bfloat16))

def partial_sum(left_rows, right_rows):
    per_index = jnp.einsum('jrd,jrf->jdf', left_rows.astype(jnp.float32), right_rows.astype(jnp.float32), precision=lax.Precision.HIGHEST)
    rounded = lax.optimization_barrier(per_index.astype(jnp.bfloat16))
    return lax.optimization_barrier(jnp.sum(rounded.astype(jnp.float32), axis=0))

def reference(section_input, saved_input, cotangent, routes_forward, gates_forward, routes_backward, gates_backward, gate_weight, up_weight, down_weight):
    blocks_count = TOKENS // TOK_DEV
    grad_scale = 1.0 / math.sqrt(GRAD_ROWS)
    mixed_list = []
    input_grads = []
    gate_grads = []
    up_grads = []
    down_grads = []
    for section_idx in range(SECTIONS):
        normed, _ = normalize(section_input[section_idx])
        slot_ids = jax.vmap(slot_table)(routes_forward[section_idx].reshape(blocks_count, TOK_DEV, TOPK))
        owners = jax.vmap(slot_owner)(slot_ids)
        padded = pad_rows(normed.astype(jnp.bfloat16).reshape(blocks_count, TOK_DEV, D))
        sent_rows = gather_rows(padded, owners).reshape(blocks_count, WINDOW, CAP, D)
        expert_outs = []
        for expert in range(WINDOW):
            produced = expert_forward(sent_rows[:, expert].reshape(-1, D), gate_weight[section_idx, expert], up_weight[section_idx, expert], down_weight[section_idx, expert])
            expert_outs.append(produced.reshape(blocks_count, CAP, D))
        returned = pad_rows(jnp.stack(expert_outs, axis=1).reshape(blocks_count, WINDOW * CAP, D))
        mixed_sum = section_input[section_idx].astype(jnp.float32).reshape(blocks_count, TOK_DEV, D)
        gate_blocks = gates_forward[section_idx].reshape(blocks_count, TOK_DEV, TOPK)
        for slot_pos in range(TOPK):
            mixed_sum = mixed_sum + gate_blocks[:, :, slot_pos, None] * gather_rows(returned, slot_ids[:, :, slot_pos]).astype(jnp.float32)
        mixed_list.append(mixed_sum.astype(jnp.bfloat16).reshape(TOKENS, D))
        saved_float, saved_scale = normalize(saved_input[section_idx])
        back_slots = jax.vmap(slot_table)(routes_backward[section_idx].reshape(blocks_count, TOK_DEV, TOPK))
        back_owners = jax.vmap(slot_owner)(back_slots)
        back_gates = jax.vmap(slot_gates)(back_slots, gates_backward[section_idx].reshape(blocks_count, TOK_DEV, TOPK))
        saved_pad = pad_rows(saved_float.astype(jnp.bfloat16).reshape(blocks_count, TOK_DEV, D))
        back_rows = gather_rows(saved_pad, back_owners).reshape(blocks_count, WINDOW, CAP, D)
        cot_pad = pad_rows(cotangent[section_idx].reshape(blocks_count, TOK_DEV, D))
        grad_rows = (back_gates[:, :, None] * gather_rows(cot_pad, back_owners).astype(jnp.float32)).astype(jnp.bfloat16)
        grad_rows = grad_rows.reshape(blocks_count, WINDOW, CAP, D)
        returned_grads = []
        section_gate = []
        section_up = []
        section_down = []
        for expert in range(WINDOW):
            rows_in = back_rows[:, expert].reshape(-1, D)
            rows_grad = grad_rows[:, expert].reshape(-1, D)
            hidden, grad_gate, grad_up, grad_input = expert_backward(rows_in, rows_grad, gate_weight[section_idx, expert], up_weight[section_idx, expert], down_weight[section_idx, expert])
            returned_grads.append(grad_input.reshape(blocks_count, CAP, D))
            left_rows = rows_in.reshape(N_DP, -1, D)
            section_gate.append(partial_sum(left_rows, grad_gate.reshape(N_DP, -1, FF)) * grad_scale)
            section_up.append(partial_sum(left_rows, grad_up.reshape(N_DP, -1, FF)) * grad_scale)
            section_down.append(partial_sum(hidden.reshape(N_DP, -1, FF), rows_grad.reshape(N_DP, -1, D)) * grad_scale)
        gate_grads.append(jnp.stack(section_gate))
        up_grads.append(jnp.stack(section_up))
        down_grads.append(jnp.stack(section_down))
        grad_table = pad_rows(jnp.stack(returned_grads, axis=1).reshape(blocks_count, WINDOW * CAP, D))
        token_grad = jnp.zeros((blocks_count, TOK_DEV, D), jnp.float32)
        for slot_pos in range(TOPK):
            token_grad = token_grad + gather_rows(grad_table, back_slots[:, :, slot_pos]).astype(jnp.float32)
        token_grad = token_grad.reshape(TOKENS, D)
        mean_term = lax.optimization_barrier(jnp.mean(saved_float * token_grad, axis=-1, keepdims=True))
        input_grad = cotangent[section_idx].astype(jnp.float32) + saved_scale * (token_grad - saved_float * mean_term)
        input_grads.append(input_grad.astype(jnp.bfloat16))
    handed = jnp.roll(jnp.stack(mixed_list), 1, axis=0)
    grad_back = jnp.roll(jnp.stack(input_grads), -1, axis=0)
    return (handed, grad_back, jnp.stack(gate_grads), jnp.stack(up_grads), jnp.stack(down_grads))
```

```python
import math

import jax
import jax.numpy as jnp
from jax import lax
from jax.experimental import pallas as pl
from jax.experimental.pallas import tpu as pltpu
from jax.sharding import PartitionSpec as P

TOPK = 8
CAP = 32
EPSILON = 1e-06
F32 = jnp.float32
BF16 = jnp.bfloat16
CONTRACT_LAST = (((1,), (1,)), ((), ()))
CONTRACT_FIRST = (((0,), (0,)), ((), ()))
VMEM_LIMIT = 56 * 1024 * 1024


def from_behind(array, axis, by):
    size = lax.axis_size(axis)
    return lax.ppermute(array, axis, [(i, (i + by) % size) for i in range(size)])


def normalize(values):
    widened = values.astype(F32)
    factor = lax.rsqrt(jnp.mean(widened * widened, axis=-1, keepdims=True) + EPSILON)
    return (widened * factor, factor)


def slot_table(listed, window):
    hit_table = (listed[:, :, None] == jnp.arange(window, dtype=jnp.int32)[None, None, :]).astype(
        jnp.int32
    )
    flat_hits = hit_table.reshape(-1, window)
    before = jnp.cumsum(flat_hits, axis=0) - flat_hits
    ranked = jnp.sum(before * flat_hits, axis=1).reshape(listed.shape)
    return jnp.where(listed < window, listed * CAP + ranked, window * CAP)


def slot_owner(slot_ids, window):
    token_total = slot_ids.shape[0]
    token_index = jnp.repeat(jnp.arange(token_total, dtype=jnp.int32), slot_ids.shape[1])
    owners = (
        jnp.full((window * CAP + 1,), token_total, jnp.int32)
        .at[slot_ids.reshape(-1)]
        .set(token_index)
    )
    return owners[: window * CAP]


def slot_gates(slot_ids, gate_vals, window):
    filled = (
        jnp.zeros((window * CAP + 1,), F32).at[slot_ids.reshape(-1)].set(gate_vals.reshape(-1))
    )
    return filled[: window * CAP]


def pad_rows(row_table):
    extra = jnp.zeros((1, row_table.shape[-1]), row_table.dtype)
    return jnp.concatenate([row_table, extra], axis=0)


def dot(a, b):
    return jnp.dot(a, b, preferred_element_type=F32)


def weights_of(w_ref):
    parts, _, half = w_ref.shape
    rows = 2 * half // parts
    low = half // parts
    gate = w_ref[:, 0:rows, :].reshape(2 * half, half)
    up = w_ref[:, rows : 2 * rows, :].reshape(2 * half, half)
    down_a = w_ref[:, 2 * rows : 2 * rows + low, :].reshape(half, half)
    down_b = w_ref[:, 2 * rows + low : 3 * rows, :].reshape(half, half)
    return gate, up, down_a, down_b


def backward_body(w_ref, r_ref, p_ref, gg_ref, gu_ref):
    gate, up, down_a, down_b = weights_of(w_ref)
    parts, _, half = w_ref.shape
    rows = 2 * half // parts
    low = half // parts
    width = 2 * half
    saved = r_ref[:, CAP : 2 * CAP, :].reshape(-1, width)
    grads = r_ref[:, 2 * CAP : 3 * CAP, :].reshape(-1, width)
    gate_act = dot(saved, gate)
    up_act = dot(saved, up)
    sigma = jax.nn.sigmoid(gate_act)
    activated = gate_act * sigma
    hidden = (activated * up_act).astype(BF16)
    p_down_a = lax.dot_general(hidden, grads[:, :half], CONTRACT_FIRST, preferred_element_type=F32)
    p_ref[:, 2 * rows : 2 * rows + low, :] = p_down_a.astype(BF16).reshape(parts, low, half)
    p_down_b = lax.dot_general(hidden, grads[:, half:], CONTRACT_FIRST, preferred_element_type=F32)
    p_ref[:, 2 * rows + low : 3 * rows, :] = p_down_b.astype(BF16).reshape(parts, low, half)
    grad_hidden = lax.dot_general(
        grads[:, :half], down_a, CONTRACT_LAST, preferred_element_type=F32
    ) + lax.dot_general(grads[:, half:], down_b, CONTRACT_LAST, preferred_element_type=F32)
    grad_gate = (grad_hidden * up_act * sigma * (1.0 + gate_act * (1.0 - sigma))).astype(BF16)
    grad_up = (grad_hidden * activated).astype(BF16)
    gg_ref[...] = grad_gate
    gu_ref[...] = grad_up
    p_gate = lax.dot_general(saved, grad_gate, CONTRACT_FIRST, preferred_element_type=F32)
    p_ref[:, 0:rows, :] = p_gate.astype(BF16).reshape(parts, rows, half)
    p_up = lax.dot_general(saved, grad_up, CONTRACT_FIRST, preferred_element_type=F32)
    p_ref[:, rows : 2 * rows, :] = p_up.astype(BF16).reshape(parts, rows, half)


def forward_body(w_ref, r_ref, gg_ref, gu_ref, o_ref):
    gate, up, down_a, down_b = weights_of(w_ref)
    half = w_ref.shape[2]
    width = 2 * half
    window = r_ref.shape[0]
    fresh = r_ref[:, 0:CAP, :].reshape(-1, width)
    gate_act = dot(fresh, gate)
    up_act = dot(fresh, up)
    hidden = (gate_act * jax.nn.sigmoid(gate_act) * up_act).astype(BF16)
    o_ref[:, 0:CAP, :half] = dot(hidden, down_a).astype(BF16).reshape(window, CAP, half)
    o_ref[:, 0:CAP, half:] = dot(hidden, down_b).astype(BF16).reshape(window, CAP, half)
    grad_input = lax.dot_general(
        gg_ref[...], gate, CONTRACT_LAST, preferred_element_type=F32
    ) + lax.dot_general(gu_ref[...], up, CONTRACT_LAST, preferred_element_type=F32)
    o_ref[:, CAP : 2 * CAP, :] = grad_input.astype(BF16).reshape(window, CAP, width)


def expert_backward(gathered, received):
    half = gathered.shape[2]
    slots = received.shape[0] * CAP
    return pl.pallas_call(
        backward_body,
        out_shape=(
            jax.ShapeDtypeStruct(gathered.shape, BF16),
            jax.ShapeDtypeStruct((slots, half), BF16),
            jax.ShapeDtypeStruct((slots, half), BF16),
        ),
        compiler_params=pltpu.CompilerParams(vmem_limit_bytes=VMEM_LIMIT),
        cost_estimate=pl.CostEstimate(
            flops=2 * slots * half * half * 2 * 6,
            bytes_accessed=8 * 1024 * 1024,
            transcendentals=slots * half,
        ),
        name="expert_backward",
    )(gathered, received)


def expert_forward(gathered, received, grad_gate, grad_up):
    half = gathered.shape[2]
    window = received.shape[0]
    slots = window * CAP
    return pl.pallas_call(
        forward_body,
        out_shape=jax.ShapeDtypeStruct((window, 2 * CAP, 2 * half), BF16),
        compiler_params=pltpu.CompilerParams(vmem_limit_bytes=VMEM_LIMIT),
        cost_estimate=pl.CostEstimate(
            flops=2 * slots * half * half * 2 * 5,
            bytes_accessed=6 * 1024 * 1024,
            transcendentals=slots * half,
        ),
        name="expert_forward",
    )(gathered, received, grad_gate, grad_up)


def local(
    section_input,
    saved_input,
    cotangent,
    routes_forward,
    gates_forward,
    routes_backward,
    gates_backward,
    gate_weight,
    up_weight,
    down_weight,
):
    window = lax.axis_size("expert")
    parts = lax.axis_size("dp")
    token_count = section_input.shape[1]
    model_width = section_input.shape[2]
    half = gate_weight.shape[3]
    rows = gate_weight.shape[2]
    low = down_weight.shape[2]

    own = jnp.concatenate(
        [
            gate_weight[0, 0],
            up_weight[0, 0],
            down_weight[0, 0, :, :half],
            down_weight[0, 0, :, half:],
        ],
        axis=0,
    )
    gathered = lax.all_gather(own, "dp", axis=0, tiled=False)

    normed, _ = normalize(section_input[0])
    slot_ids = slot_table(routes_forward[0], window)
    owners = slot_owner(slot_ids, window)
    sent_forward = pad_rows(normed.astype(BF16))[owners].reshape(window, CAP, model_width)
    saved_float, saved_scale = normalize(saved_input[0])
    back_slots = slot_table(routes_backward[0], window)
    back_owners = slot_owner(back_slots, window)
    back_gates = slot_gates(back_slots, gates_backward[0], window)
    sent_backward = pad_rows(saved_float.astype(BF16))[back_owners].reshape(
        window, CAP, model_width
    )
    grad_sent = (back_gates[:, None] * pad_rows(cotangent[0])[back_owners].astype(F32)).astype(BF16)
    grad_sent = grad_sent.reshape(window, CAP, model_width)
    sent = jnp.concatenate([sent_forward, sent_backward, grad_sent], axis=1)
    received = lax.all_to_all(sent, "expert", split_axis=0, concat_axis=0, tiled=True)

    partial, grad_gate, grad_up = expert_backward(gathered, received)
    summed = lax.psum_scatter(
        partial.reshape(parts * 3 * rows, half), "dp", scatter_dimension=0, tiled=True
    )

    produced = expert_forward(gathered, received, grad_gate, grad_up)
    home = lax.all_to_all(produced, "expert", split_axis=0, concat_axis=0, tiled=True)

    returned_pad = pad_rows(home[:, :CAP].reshape(window * CAP, model_width))
    mixed_sum = section_input[0].astype(F32)
    for slot_pos in range(TOPK):
        mixed_sum = mixed_sum + gates_forward[0][:, slot_pos, None] * returned_pad[
            slot_ids[:, slot_pos]
        ].astype(F32)
    handed = from_behind(mixed_sum.astype(BF16)[None], "section", 1)
    grad_pad = pad_rows(home[:, CAP:].reshape(window * CAP, model_width))
    token_grad = jnp.zeros((token_count, model_width), F32)
    for slot_pos in range(TOPK):
        token_grad = token_grad + grad_pad[back_slots[:, slot_pos]].astype(F32)
    mean_term = jnp.mean(saved_float * token_grad, axis=-1, keepdims=True)
    input_grad = cotangent[0].astype(F32) + saved_scale * (token_grad - saved_float * mean_term)
    grad_back = from_behind(input_grad.astype(BF16)[None], "section", -1)

    grad_scale = 1.0 / math.sqrt(parts * token_count)
    scaled = summed.astype(F32) * grad_scale
    grad_gate_out = scaled[:rows][None, None]
    grad_up_out = scaled[rows : 2 * rows][None, None]
    grad_down_out = jnp.concatenate(
        [scaled[2 * rows : 2 * rows + low], scaled[2 * rows + low :]], axis=1
    )[None, None]
    return (handed, grad_back, grad_gate_out, grad_up_out, grad_down_out)


def solution(mesh):
    tokens = P("section", ("dp", "expert"), None)
    weights = P("section", "expert", "dp", None)
    return jax.shard_map(
        local,
        mesh=mesh,
        in_specs=(tokens,) * 7 + (weights,) * 3,
        out_specs=(tokens,) * 2 + (weights,) * 3,
        check_vma=False,
    )
```

```python
import functools
import math

import jax
import jax.numpy as jnp
from jax import lax
from jax.experimental import pallas as pl
from jax.experimental.pallas import tpu as pltpu
from jax.sharding import PartitionSpec as P

TOPK = 8
CAP = 32
EPSILON = 1e-06
F32 = jnp.float32
BF16 = jnp.bfloat16
CONTRACT_LAST = (((1,), (1,)), ((), ()))
CONTRACT_FIRST = (((0,), (0,)), ((), ()))
VMEM_LIMIT = 56 * 1024 * 1024


def from_behind(array, axis, by):
    size = lax.axis_size(axis)
    return lax.ppermute(array, axis, [(i, (i + by) % size) for i in range(size)])


def normalize(values):
    widened = values.astype(F32)
    factor = lax.rsqrt(jnp.mean(widened * widened, axis=-1, keepdims=True) + EPSILON)
    return (widened * factor, factor)


def slot_table(listed, window):
    hit_table = (listed[:, :, None] == jnp.arange(window, dtype=jnp.int32)[None, None, :]).astype(
        jnp.int32
    )
    flat_hits = hit_table.reshape(-1, window)
    before = jnp.cumsum(flat_hits, axis=0) - flat_hits
    ranked = jnp.sum(before * flat_hits, axis=1).reshape(listed.shape)
    return jnp.where(listed < window, listed * CAP + ranked, window * CAP)


def slot_owner(slot_ids, window):
    token_total = slot_ids.shape[0]
    token_index = jnp.repeat(jnp.arange(token_total, dtype=jnp.int32), slot_ids.shape[1])
    owners = (
        jnp.full((window * CAP + 1,), token_total, jnp.int32)
        .at[slot_ids.reshape(-1)]
        .set(token_index)
    )
    return owners[: window * CAP]


def slot_gates(slot_ids, gate_vals, window):
    filled = (
        jnp.zeros((window * CAP + 1,), F32).at[slot_ids.reshape(-1)].set(gate_vals.reshape(-1))
    )
    return filled[: window * CAP]


def pad_rows(row_table):
    extra = jnp.zeros((1, row_table.shape[-1]), row_table.dtype)
    return jnp.concatenate([row_table, extra], axis=0)


def dot(a, b):
    return jnp.dot(a, b, preferred_element_type=F32)


CHUNK = 4


def pack_body(gate_ref, up_ref, down_ref, own_ref):
    rows, half = gate_ref.shape
    own_ref[0:rows, 0:half] = gate_ref[...]
    own_ref[0:rows, half:] = up_ref[...]
    own_ref[rows:, :] = down_ref[...]


def unpack_body(scale, summed_ref, gate_ref, up_ref, down_ref):
    rows, half = gate_ref.shape
    gate_ref[...] = summed_ref[0:rows, 0:half].astype(F32) * scale
    up_ref[...] = summed_ref[0:rows, half:].astype(F32) * scale
    down_ref[...] = summed_ref[rows:, :].astype(F32) * scale


def land_body(a_ref, b_ref, x_ref, y_ref):
    x_ref[...] = a_ref[...]
    y_ref[...] = b_ref[...]


def backward_body(
    w_hbm, r_hbm, p_hbm, g_hbm, first_v, down_v, saved_v, grads_v, act_v, pd_v, pg_v, g_v, sem
):
    parts, block, width = w_hbm.shape
    half = width // 2
    rows = width // parts
    chunks = parts // CHUNK
    span = CHUNK * rows
    window = r_hbm.shape[0]
    slots = window * CAP
    load_saved = pltpu.make_async_copy(r_hbm.at[:, CAP : 2 * CAP, :], saved_v, sem.at[0])
    load_saved.start()
    loads = []
    for c in range(chunks):
        copy = pltpu.make_async_copy(
            w_hbm.at[c * CHUNK : (c + 1) * CHUNK, 0:rows, :], first_v.at[c], sem.at[3 + c]
        )
        copy.start()
        loads.append(copy)
    load_grads = pltpu.make_async_copy(r_hbm.at[:, 2 * CAP : 3 * CAP, :], grads_v, sem.at[1])
    load_grads.start()
    load_down = pltpu.make_async_copy(w_hbm.at[:, rows:block, :], down_v, sem.at[2])
    load_down.start()
    load_saved.wait()
    saved = saved_v[...].reshape(slots, width)
    for c in range(chunks):
        loads[c].wait()
        part = dot(saved[:, c * span : (c + 1) * span], first_v[c].reshape(span, width))
        act_v[...] = part if c == 0 else act_v[...] + part
    gate_act = act_v[:, :half]
    up_act = act_v[:, half:]
    sigma = jax.nn.sigmoid(gate_act)
    activated = gate_act * sigma
    hidden = (activated * up_act).astype(BF16)
    load_grads.wait()
    grads = grads_v[...].reshape(slots, width)
    p_down = lax.dot_general(hidden, grads, CONTRACT_FIRST, preferred_element_type=F32)
    pd_v[...] = p_down.astype(BF16).reshape(pd_v.shape)
    stores = [pltpu.make_async_copy(pd_v, p_hbm.at[:, rows:block, :], sem.at[3 + chunks])]
    stores[0].start()
    load_down.wait()
    down = down_v[...].reshape(half, width)
    grad_hidden = lax.dot_general(grads, down, CONTRACT_LAST, preferred_element_type=F32)
    grad_gate = (grad_hidden * up_act * sigma * (1.0 + gate_act * (1.0 - sigma))).astype(BF16)
    grad_up = (grad_hidden * activated).astype(BF16)
    g_v[:, :half] = grad_gate
    g_v[:, half:] = grad_up
    store_g = pltpu.make_async_copy(g_v, g_hbm, sem.at[4 + chunks])
    store_g.start()
    both = g_v[...]
    for c in range(chunks):
        part = lax.dot_general(
            saved[:, c * span : (c + 1) * span], both, CONTRACT_FIRST, preferred_element_type=F32
        )
        pg_v[c] = part.astype(BF16).reshape(CHUNK, rows, width)
        copy = pltpu.make_async_copy(
            pg_v.at[c], p_hbm.at[c * CHUNK : (c + 1) * CHUNK, 0:rows, :], sem.at[5 + chunks + c]
        )
        copy.start()
        stores.append(copy)
    store_g.wait()
    for copy in stores:
        copy.wait()


def forward_body(w_ref, r_ref, g_ref, o_ref):
    parts, block, width = w_ref.shape
    half = width // 2
    rows = width // parts
    window = r_ref.shape[0]
    first = w_ref[:, 0:rows, :].reshape(width, width)
    down = w_ref[:, rows:block, :].reshape(half, width)
    fresh = r_ref[:, 0:CAP, :].reshape(-1, width)
    act = dot(fresh, first)
    gate_act = act[:, :half]
    hidden = (gate_act * jax.nn.sigmoid(gate_act) * act[:, half:]).astype(BF16)
    o_ref[:, 0:CAP, :] = dot(hidden, down).astype(BF16).reshape(window, CAP, width)
    grad_input = lax.dot_general(g_ref[...], first, CONTRACT_LAST, preferred_element_type=F32)
    o_ref[:, CAP : 2 * CAP, :] = grad_input.astype(BF16).reshape(window, CAP, width)


def pack(gate, up, down):
    rows, half = gate.shape
    return pl.pallas_call(
        pack_body,
        out_shape=jax.ShapeDtypeStruct((rows + down.shape[0], 2 * half), BF16),
        name="pack_weights",
    )(gate, up, down)


def unpack(summed, rows, low, half, scale):
    return pl.pallas_call(
        functools.partial(unpack_body, scale),
        out_shape=(
            jax.ShapeDtypeStruct((rows, half), F32),
            jax.ShapeDtypeStruct((rows, half), F32),
            jax.ShapeDtypeStruct((low, 2 * half), F32),
        ),
        name="unpack_grads",
    )(summed)


def land(a, b):
    return pl.pallas_call(
        land_body,
        out_shape=(jax.ShapeDtypeStruct(a.shape, BF16), jax.ShapeDtypeStruct(b.shape, BF16)),
        cost_estimate=pl.CostEstimate(flops=0, bytes_accessed=1 << 20, transcendentals=0),
        name="land",
    )(a, b)


def expert_backward(gathered, received):
    parts, block, width = gathered.shape
    half = width // 2
    rows = width // parts
    chunks = parts // CHUNK
    window = received.shape[0]
    slots = window * CAP
    anywhere = pl.BlockSpec(memory_space=pl.ANY)
    return pl.pallas_call(
        backward_body,
        in_specs=[anywhere, anywhere],
        out_specs=(anywhere, anywhere),
        out_shape=(
            jax.ShapeDtypeStruct(gathered.shape, BF16),
            jax.ShapeDtypeStruct((slots, width), BF16),
        ),
        scratch_shapes=[
            pltpu.VMEM((chunks, CHUNK, rows, width), BF16),
            pltpu.VMEM((parts, block - rows, width), BF16),
            pltpu.VMEM((window, CAP, width), BF16),
            pltpu.VMEM((window, CAP, width), BF16),
            pltpu.VMEM((slots, width), F32),
            pltpu.VMEM((parts, block - rows, width), BF16),
            pltpu.VMEM((chunks, CHUNK, rows, width), BF16),
            pltpu.VMEM((slots, width), BF16),
            pltpu.SemaphoreType.DMA((5 + 2 * chunks,)),
        ],
        compiler_params=pltpu.CompilerParams(vmem_limit_bytes=VMEM_LIMIT),
        cost_estimate=pl.CostEstimate(
            flops=2 * slots * half * width * 6,
            bytes_accessed=8 * 1024 * 1024,
            transcendentals=slots * half,
        ),
        name="expert_backward",
    )(gathered, received)


def expert_forward(gathered, received, grads):
    width = gathered.shape[2]
    window = received.shape[0]
    slots = window * CAP
    return pl.pallas_call(
        forward_body,
        out_shape=jax.ShapeDtypeStruct((window, 2 * CAP, width), BF16),
        compiler_params=pltpu.CompilerParams(vmem_limit_bytes=VMEM_LIMIT),
        cost_estimate=pl.CostEstimate(
            flops=slots * width * width * 5,
            bytes_accessed=6 * 1024 * 1024,
            transcendentals=slots * width // 2,
        ),
        name="expert_forward",
    )(gathered, received, grads)


def local(
    section_input,
    saved_input,
    cotangent,
    routes_forward,
    gates_forward,
    routes_backward,
    gates_backward,
    gate_weight,
    up_weight,
    down_weight,
):
    window = lax.axis_size("expert")
    parts = lax.axis_size("dp")
    token_count = section_input.shape[1]
    model_width = section_input.shape[2]
    half = gate_weight.shape[3]
    rows = gate_weight.shape[2]
    low = down_weight.shape[2]

    own = pack(gate_weight[0, 0], up_weight[0, 0], down_weight[0, 0])
    gathered = lax.all_gather(own, "dp", axis=0, tiled=False)

    normed, _ = normalize(section_input[0])
    slot_ids = slot_table(routes_forward[0], window)
    owners = slot_owner(slot_ids, window)
    sent_forward = pad_rows(normed.astype(BF16))[owners].reshape(window, CAP, model_width)
    saved_float, saved_scale = normalize(saved_input[0])
    back_slots = slot_table(routes_backward[0], window)
    back_owners = slot_owner(back_slots, window)
    back_gates = slot_gates(back_slots, gates_backward[0], window)
    sent_backward = pad_rows(saved_float.astype(BF16))[back_owners].reshape(
        window, CAP, model_width
    )
    grad_sent = (back_gates[:, None] * pad_rows(cotangent[0])[back_owners].astype(F32)).astype(BF16)
    grad_sent = grad_sent.reshape(window, CAP, model_width)
    sent = jnp.concatenate([sent_forward, sent_backward, grad_sent], axis=1)
    received = lax.all_to_all(sent, "expert", split_axis=0, concat_axis=0, tiled=True)

    partial, act_grads = expert_backward(gathered, received)
    summed = lax.psum_scatter(
        partial.reshape(parts * (rows + low), model_width), "dp", scatter_dimension=0, tiled=True
    )

    produced = expert_forward(gathered, received, act_grads)
    home = lax.all_to_all(produced, "expert", split_axis=0, concat_axis=0, tiled=True)

    returned_pad = pad_rows(home[:, :CAP].reshape(window * CAP, model_width))
    mixed_sum = section_input[0].astype(F32)
    for slot_pos in range(TOPK):
        mixed_sum = mixed_sum + gates_forward[0][:, slot_pos, None] * returned_pad[
            slot_ids[:, slot_pos]
        ].astype(F32)
    handed = from_behind(mixed_sum.astype(BF16)[None], "section", 1)
    grad_pad = pad_rows(home[:, CAP:].reshape(window * CAP, model_width))
    token_grad = jnp.zeros((token_count, model_width), F32)
    for slot_pos in range(TOPK):
        token_grad = token_grad + grad_pad[back_slots[:, slot_pos]].astype(F32)
    mean_term = jnp.mean(saved_float * token_grad, axis=-1, keepdims=True)
    input_grad = cotangent[0].astype(F32) + saved_scale * (token_grad - saved_float * mean_term)
    grad_back = from_behind(input_grad.astype(BF16)[None], "section", -1)

    handed, grad_back = land(handed, grad_back)
    grad_scale = 1.0 / math.sqrt(parts * token_count)
    grad_gate, grad_up, grad_down = unpack(summed, rows, low, half, grad_scale)
    return (
        handed,
        grad_back,
        grad_gate[None, None],
        grad_up[None, None],
        grad_down[None, None],
    )


def solution(mesh):
    tokens = P("section", ("dp", "expert"), None)
    weights = P("section", "expert", "dp", None)
    return jax.shard_map(
        local,
        mesh=mesh,
        in_specs=(tokens,) * 7 + (weights,) * 3,
        out_specs=(tokens,) * 2 + (weights,) * 3,
        check_vma=False,
    )
```

```python
import functools
import math

import jax
import jax.numpy as jnp
from jax import lax
from jax.experimental import pallas as pl
from jax.experimental.pallas import tpu as pltpu
from jax.sharding import PartitionSpec as P

TOPK = 8
CAP = 32
EPSILON = 1e-06
F32 = jnp.float32
BF16 = jnp.bfloat16
CONTRACT_LAST = (((1,), (1,)), ((), ()))
CONTRACT_FIRST = (((0,), (0,)), ((), ()))
VMEM_LIMIT = 56 * 1024 * 1024


def from_behind(array, axis, by):
    size = lax.axis_size(axis)
    return lax.ppermute(array, axis, [(i, (i + by) % size) for i in range(size)])


def crossed(expert, index):
    return expert ^ (index & 1)


def cross_rings():
    parts, window = lax.axis_size("dp"), lax.axis_size("expert")
    return [[d * window + crossed(e, d) for d in range(parts)] for e in range(window)]


def cross_swap(array):
    parts, window = lax.axis_size("dp"), lax.axis_size("expert")
    pairs = [
        (d * window + e, d * window + crossed(e, d)) for d in range(parts) for e in range(window)
    ]
    return lax.ppermute(array, ("dp", "expert"), pairs)


def normalize(values):
    widened = values.astype(F32)
    factor = lax.rsqrt(jnp.mean(widened * widened, axis=-1, keepdims=True) + EPSILON)
    return (widened * factor, factor)


def slot_table(listed, window):
    hit_table = (listed[:, :, None] == jnp.arange(window, dtype=jnp.int32)[None, None, :]).astype(
        jnp.int32
    )
    flat_hits = hit_table.reshape(-1, window)
    before = jnp.cumsum(flat_hits, axis=0) - flat_hits
    ranked = jnp.sum(before * flat_hits, axis=1).reshape(listed.shape)
    return jnp.where(listed < window, listed * CAP + ranked, window * CAP)


def slot_owner(slot_ids, window):
    token_total = slot_ids.shape[0]
    token_index = jnp.repeat(jnp.arange(token_total, dtype=jnp.int32), slot_ids.shape[1])
    owners = (
        jnp.full((window * CAP + 1,), token_total, jnp.int32)
        .at[slot_ids.reshape(-1)]
        .set(token_index)
    )
    return owners[: window * CAP]


def slot_gates(slot_ids, gate_vals, window):
    filled = (
        jnp.zeros((window * CAP + 1,), F32).at[slot_ids.reshape(-1)].set(gate_vals.reshape(-1))
    )
    return filled[: window * CAP]


def pad_rows(row_table):
    extra = jnp.zeros((1, row_table.shape[-1]), row_table.dtype)
    return jnp.concatenate([row_table, extra], axis=0)


def dot(a, b):
    return jnp.dot(a, b, preferred_element_type=F32)


CHUNK = 4


def pack_body(gate_ref, up_ref, down_ref, own_ref):
    rows, half = gate_ref.shape
    own_ref[0:rows, 0:half] = gate_ref[...]
    own_ref[0:rows, half:] = up_ref[...]
    own_ref[rows:, :] = down_ref[...]


def unpack_body(scale, summed_ref, gate_ref, up_ref, down_ref):
    rows, half = gate_ref.shape
    gate_ref[...] = summed_ref[0:rows, 0:half].astype(F32) * scale
    up_ref[...] = summed_ref[0:rows, half:].astype(F32) * scale
    down_ref[...] = summed_ref[rows:, :].astype(F32) * scale


def land_body(a_ref, b_ref, x_ref, y_ref):
    x_ref[...] = a_ref[...]
    y_ref[...] = b_ref[...]


def backward_body(
    w_hbm, r_hbm, p_hbm, g_hbm, first_v, down_v, saved_v, grads_v, act_v, pd_v, pg_v, g_v, sem
):
    parts, block, width = w_hbm.shape
    half = width // 2
    rows = width // parts
    chunks = parts // CHUNK
    span = CHUNK * rows
    window = r_hbm.shape[0]
    slots = window * CAP
    load_saved = pltpu.make_async_copy(r_hbm.at[:, CAP : 2 * CAP, :], saved_v, sem.at[0])
    load_saved.start()
    loads = []
    for c in range(chunks):
        copy = pltpu.make_async_copy(
            w_hbm.at[c * CHUNK : (c + 1) * CHUNK, 0:rows, :], first_v.at[c], sem.at[3 + c]
        )
        copy.start()
        loads.append(copy)
    load_grads = pltpu.make_async_copy(r_hbm.at[:, 2 * CAP : 3 * CAP, :], grads_v, sem.at[1])
    load_grads.start()
    load_down = pltpu.make_async_copy(w_hbm.at[:, rows:block, :], down_v, sem.at[2])
    load_down.start()
    load_saved.wait()
    saved = saved_v[...].reshape(slots, width)
    for c in range(chunks):
        loads[c].wait()
        part = dot(saved[:, c * span : (c + 1) * span], first_v[c].reshape(span, width))
        act_v[...] = part if c == 0 else act_v[...] + part
    gate_act = act_v[:, :half]
    up_act = act_v[:, half:]
    sigma = jax.nn.sigmoid(gate_act)
    activated = gate_act * sigma
    hidden = (activated * up_act).astype(BF16)
    load_grads.wait()
    grads = grads_v[...].reshape(slots, width)
    p_down = lax.dot_general(hidden, grads, CONTRACT_FIRST, preferred_element_type=F32)
    pd_v[...] = p_down.astype(BF16).reshape(pd_v.shape)
    stores = [pltpu.make_async_copy(pd_v, p_hbm.at[:, rows:block, :], sem.at[3 + chunks])]
    stores[0].start()
    load_down.wait()
    down = down_v[...].reshape(half, width)
    grad_hidden = lax.dot_general(grads, down, CONTRACT_LAST, preferred_element_type=F32)
    grad_gate = (grad_hidden * up_act * sigma * (1.0 + gate_act * (1.0 - sigma))).astype(BF16)
    grad_up = (grad_hidden * activated).astype(BF16)
    g_v[:, :half] = grad_gate
    g_v[:, half:] = grad_up
    store_g = pltpu.make_async_copy(g_v, g_hbm, sem.at[4 + chunks])
    store_g.start()
    both = g_v[...]
    for c in range(chunks):
        part = lax.dot_general(
            saved[:, c * span : (c + 1) * span], both, CONTRACT_FIRST, preferred_element_type=F32
        )
        pg_v[c] = part.astype(BF16).reshape(CHUNK, rows, width)
        copy = pltpu.make_async_copy(
            pg_v.at[c], p_hbm.at[c * CHUNK : (c + 1) * CHUNK, 0:rows, :], sem.at[5 + chunks + c]
        )
        copy.start()
        stores.append(copy)
    store_g.wait()
    for copy in stores:
        copy.wait()


def forward_body(w_ref, r_ref, g_ref, o_ref):
    parts, block, width = w_ref.shape
    half = width // 2
    rows = width // parts
    window = r_ref.shape[0]
    first = w_ref[:, 0:rows, :].reshape(width, width)
    down = w_ref[:, rows:block, :].reshape(half, width)
    fresh = r_ref[:, 0:CAP, :].reshape(-1, width)
    act = dot(fresh, first)
    gate_act = act[:, :half]
    hidden = (gate_act * jax.nn.sigmoid(gate_act) * act[:, half:]).astype(BF16)
    o_ref[:, 0:CAP, :] = dot(hidden, down).astype(BF16).reshape(window, CAP, width)
    grad_input = lax.dot_general(g_ref[...], first, CONTRACT_LAST, preferred_element_type=F32)
    o_ref[:, CAP : 2 * CAP, :] = grad_input.astype(BF16).reshape(window, CAP, width)


def pack(gate, up, down):
    rows, half = gate.shape
    return pl.pallas_call(
        pack_body,
        out_shape=jax.ShapeDtypeStruct((rows + down.shape[0], 2 * half), BF16),
        name="pack_weights",
    )(gate, up, down)


def unpack(summed, rows, low, half, scale):
    return pl.pallas_call(
        functools.partial(unpack_body, scale),
        out_shape=(
            jax.ShapeDtypeStruct((rows, half), F32),
            jax.ShapeDtypeStruct((rows, half), F32),
            jax.ShapeDtypeStruct((low, 2 * half), F32),
        ),
        compiler_params=pltpu.CompilerParams(vmem_limit_bytes=8 * 1024 * 1024),
        name="unpack_grads",
    )(summed)


def land(a, b):
    return pl.pallas_call(
        land_body,
        out_shape=(jax.ShapeDtypeStruct(a.shape, BF16), jax.ShapeDtypeStruct(b.shape, BF16)),
        cost_estimate=pl.CostEstimate(flops=0, bytes_accessed=1 << 20, transcendentals=0),
        name="land",
    )(a, b)


def expert_backward(gathered, received):
    parts, block, width = gathered.shape
    half = width // 2
    rows = width // parts
    chunks = parts // CHUNK
    window = received.shape[0]
    slots = window * CAP
    anywhere = pl.BlockSpec(memory_space=pl.ANY)
    return pl.pallas_call(
        backward_body,
        in_specs=[anywhere, anywhere],
        out_specs=(anywhere, anywhere),
        out_shape=(
            jax.ShapeDtypeStruct(gathered.shape, BF16),
            jax.ShapeDtypeStruct((slots, width), BF16),
        ),
        scratch_shapes=[
            pltpu.VMEM((chunks, CHUNK, rows, width), BF16),
            pltpu.VMEM((parts, block - rows, width), BF16),
            pltpu.VMEM((window, CAP, width), BF16),
            pltpu.VMEM((window, CAP, width), BF16),
            pltpu.VMEM((slots, width), F32),
            pltpu.VMEM((parts, block - rows, width), BF16),
            pltpu.VMEM((chunks, CHUNK, rows, width), BF16),
            pltpu.VMEM((slots, width), BF16),
            pltpu.SemaphoreType.DMA((5 + 2 * chunks,)),
        ],
        compiler_params=pltpu.CompilerParams(vmem_limit_bytes=VMEM_LIMIT),
        cost_estimate=pl.CostEstimate(
            flops=2 * slots * half * width * 6,
            bytes_accessed=8 * 1024 * 1024,
            transcendentals=slots * half,
        ),
        name="expert_backward",
    )(gathered, received)


def expert_forward(gathered, received, grads):
    width = gathered.shape[2]
    window = received.shape[0]
    slots = window * CAP
    return pl.pallas_call(
        forward_body,
        out_shape=jax.ShapeDtypeStruct((window, 2 * CAP, width), BF16),
        compiler_params=pltpu.CompilerParams(vmem_limit_bytes=VMEM_LIMIT),
        cost_estimate=pl.CostEstimate(
            flops=slots * width * width * 5,
            bytes_accessed=6 * 1024 * 1024,
            transcendentals=slots * width // 2,
        ),
        name="expert_forward",
    )(gathered, received, grads)


def local(
    section_input,
    saved_input,
    cotangent,
    routes_forward,
    gates_forward,
    routes_backward,
    gates_backward,
    gate_weight,
    up_weight,
    down_weight,
):
    window = lax.axis_size("expert")
    parts = lax.axis_size("dp")
    token_count = section_input.shape[1]
    model_width = section_input.shape[2]
    half = gate_weight.shape[3]
    rows = gate_weight.shape[2]
    low = down_weight.shape[2]

    own = pack(gate_weight[0, 0], up_weight[0, 0], down_weight[0, 0])
    index = lax.axis_index("dp")
    own = cross_swap(own)
    own, section_input, saved_input, cotangent, routes_forward, routes_backward, gates_backward = (
        lax.optimization_barrier(
            (
                own,
                section_input,
                saved_input,
                cotangent,
                routes_forward,
                routes_backward,
                gates_backward,
            )
        )
    )
    gathered = lax.all_gather(
        own,
        ("dp", "expert"),
        axis=0,
        tiled=True,
        axis_index_groups=cross_rings(),
    ).reshape(parts, rows + low, model_width)

    normed, _ = normalize(section_input[0])
    slot_ids = slot_table(crossed(routes_forward[0], index), window)
    owners = slot_owner(slot_ids, window)
    sent_forward = pad_rows(normed.astype(BF16))[owners].reshape(window, CAP, model_width)
    saved_float, saved_scale = normalize(saved_input[0])
    back_slots = slot_table(crossed(routes_backward[0], index), window)
    back_owners = slot_owner(back_slots, window)
    back_gates = slot_gates(back_slots, gates_backward[0], window)
    sent_backward = pad_rows(saved_float.astype(BF16))[back_owners].reshape(
        window, CAP, model_width
    )
    grad_sent = (back_gates[:, None] * pad_rows(cotangent[0])[back_owners].astype(F32)).astype(BF16)
    grad_sent = grad_sent.reshape(window, CAP, model_width)
    sent = jnp.concatenate([sent_forward, sent_backward, grad_sent], axis=1)
    received = lax.all_to_all(sent, "expert", split_axis=0, concat_axis=0, tiled=True)

    partial, act_grads = expert_backward(gathered, received)
    summed = lax.psum_scatter(
        partial.reshape(parts * (rows + low), model_width),
        ("dp", "expert"),
        scatter_dimension=0,
        axis_index_groups=cross_rings(),
        tiled=True,
    )

    produced = expert_forward(gathered, received, act_grads)
    home = lax.all_to_all(produced, "expert", split_axis=0, concat_axis=0, tiled=True)

    returned_pad = pad_rows(home[:, :CAP].reshape(window * CAP, model_width))
    mixed_sum = section_input[0].astype(F32)
    for slot_pos in range(TOPK):
        mixed_sum = mixed_sum + gates_forward[0][:, slot_pos, None] * returned_pad[
            slot_ids[:, slot_pos]
        ].astype(F32)
    handed = from_behind(mixed_sum.astype(BF16)[None], "section", 1)
    grad_pad = pad_rows(home[:, CAP:].reshape(window * CAP, model_width))
    token_grad = jnp.zeros((token_count, model_width), F32)
    for slot_pos in range(TOPK):
        token_grad = token_grad + grad_pad[back_slots[:, slot_pos]].astype(F32)
    mean_term = jnp.mean(saved_float * token_grad, axis=-1, keepdims=True)
    input_grad = cotangent[0].astype(F32) + saved_scale * (token_grad - saved_float * mean_term)
    grad_back = from_behind(input_grad.astype(BF16)[None], "section", -1)

    handed, grad_back = land(handed, grad_back)
    summed, handed, grad_back = lax.optimization_barrier((summed, handed, grad_back))
    summed = cross_swap(summed)
    grad_scale = 1.0 / math.sqrt(parts * token_count)
    grad_gate, grad_up, grad_down = unpack(summed, rows, low, half, grad_scale)
    return (
        handed,
        grad_back,
        grad_gate[None, None],
        grad_up[None, None],
        grad_down[None, None],
    )


def solution(mesh):
    tokens = P("section", ("dp", "expert"), None)
    weights = P("section", "expert", "dp", None)
    return jax.shard_map(
        local,
        mesh=mesh,
        in_specs=(tokens,) * 7 + (weights,) * 3,
        out_specs=(tokens,) * 2 + (weights,) * 3,
        check_vma=False,
    )
```

```python
import functools
import math

import jax
import jax.numpy as jnp
from jax import lax
from jax.experimental import pallas as pl
from jax.experimental.pallas import tpu as pltpu
from jax.sharding import PartitionSpec as P

TOPK = 8
CAP = 32
EPSILON = 1e-06
F32 = jnp.float32
BF16 = jnp.bfloat16
CONTRACT_LAST = (((1,), (1,)), ((), ()))
CONTRACT_FIRST = (((0,), (0,)), ((), ()))
VMEM_LIMIT = 56 * 1024 * 1024


def from_behind(array, axis, by):
    size = lax.axis_size(axis)
    return lax.ppermute(array, axis, [(i, (i + by) % size) for i in range(size)])


def crossed(expert, index):
    half = lax.axis_size("dp") // 2
    return expert ^ (1 - index // half)


def cross_rings():
    parts, window = lax.axis_size("dp"), lax.axis_size("expert")
    return [[d * window + crossed(e, d) for d in range(parts)] for e in range(window)]


def cross_swap(array):
    parts, window = lax.axis_size("dp"), lax.axis_size("expert")
    pairs = [
        (d * window + e, d * window + crossed(e, d)) for d in range(parts) for e in range(window)
    ]
    return lax.ppermute(array, ("dp", "expert"), pairs)


def normalize(values):
    widened = values.astype(F32)
    factor = lax.rsqrt(jnp.mean(widened * widened, axis=-1, keepdims=True) + EPSILON)
    return (widened * factor, factor)


def slot_table(listed, window):
    hit_table = (listed[:, :, None] == jnp.arange(window, dtype=jnp.int32)[None, None, :]).astype(
        jnp.int32
    )
    flat_hits = hit_table.reshape(-1, window)
    before = jnp.cumsum(flat_hits, axis=0) - flat_hits
    ranked = jnp.sum(before * flat_hits, axis=1).reshape(listed.shape)
    return jnp.where(listed < window, listed * CAP + ranked, window * CAP)


def slot_owner(slot_ids, window):
    token_total = slot_ids.shape[0]
    token_index = jnp.repeat(jnp.arange(token_total, dtype=jnp.int32), slot_ids.shape[1])
    owners = (
        jnp.full((window * CAP + 1,), token_total, jnp.int32)
        .at[slot_ids.reshape(-1)]
        .set(token_index)
    )
    return owners[: window * CAP]


def slot_gates(slot_ids, gate_vals, window):
    filled = (
        jnp.zeros((window * CAP + 1,), F32).at[slot_ids.reshape(-1)].set(gate_vals.reshape(-1))
    )
    return filled[: window * CAP]


def pad_rows(row_table):
    extra = jnp.zeros((1, row_table.shape[-1]), row_table.dtype)
    return jnp.concatenate([row_table, extra], axis=0)


def dot(a, b):
    return jnp.dot(a, b, preferred_element_type=F32)


CHUNK = 4


def pack_body(gate_ref, up_ref, down_ref, own_ref):
    rows, half = gate_ref.shape
    own_ref[0:rows, 0:half] = gate_ref[...]
    own_ref[0:rows, half:] = up_ref[...]
    own_ref[rows:, :] = down_ref[...]


def unpack_body(scale, summed_ref, gate_ref, up_ref, down_ref):
    rows, half = gate_ref.shape
    gate_ref[...] = summed_ref[0:rows, 0:half].astype(F32) * scale
    up_ref[...] = summed_ref[0:rows, half:].astype(F32) * scale
    down_ref[...] = summed_ref[rows:, :].astype(F32) * scale


def land_body(a_ref, b_ref, x_ref, y_ref):
    x_ref[...] = a_ref[...]
    y_ref[...] = b_ref[...]


def backward_body(
    w_hbm, r_hbm, p_hbm, g_hbm, first_v, down_v, saved_v, grads_v, act_v, pd_v, pg_v, g_v, sem
):
    parts, block, width = w_hbm.shape
    half = width // 2
    rows = width // parts
    chunks = parts // CHUNK
    span = CHUNK * rows
    window = r_hbm.shape[0]
    slots = window * CAP
    load_saved = pltpu.make_async_copy(r_hbm.at[:, CAP : 2 * CAP, :], saved_v, sem.at[0])
    load_saved.start()
    loads = []
    for c in range(chunks):
        copy = pltpu.make_async_copy(
            w_hbm.at[c * CHUNK : (c + 1) * CHUNK, 0:rows, :], first_v.at[c], sem.at[3 + c]
        )
        copy.start()
        loads.append(copy)
    load_grads = pltpu.make_async_copy(r_hbm.at[:, 2 * CAP : 3 * CAP, :], grads_v, sem.at[1])
    load_grads.start()
    load_down = pltpu.make_async_copy(w_hbm.at[:, rows:block, :], down_v, sem.at[2])
    load_down.start()
    load_saved.wait()
    saved = saved_v[...].reshape(slots, width)
    for c in range(chunks):
        loads[c].wait()
        part = dot(saved[:, c * span : (c + 1) * span], first_v[c].reshape(span, width))
        act_v[...] = part if c == 0 else act_v[...] + part
    gate_act = act_v[:, :half]
    up_act = act_v[:, half:]
    sigma = jax.nn.sigmoid(gate_act)
    activated = gate_act * sigma
    hidden = (activated * up_act).astype(BF16)
    load_grads.wait()
    grads = grads_v[...].reshape(slots, width)
    p_down = lax.dot_general(hidden, grads, CONTRACT_FIRST, preferred_element_type=F32)
    pd_v[...] = p_down.astype(BF16).reshape(pd_v.shape)
    stores = [pltpu.make_async_copy(pd_v, p_hbm.at[:, rows:block, :], sem.at[3 + chunks])]
    stores[0].start()
    load_down.wait()
    down = down_v[...].reshape(half, width)
    grad_hidden = lax.dot_general(grads, down, CONTRACT_LAST, preferred_element_type=F32)
    grad_gate = (grad_hidden * up_act * sigma * (1.0 + gate_act * (1.0 - sigma))).astype(BF16)
    grad_up = (grad_hidden * activated).astype(BF16)
    g_v[:, :half] = grad_gate
    g_v[:, half:] = grad_up
    store_g = pltpu.make_async_copy(g_v, g_hbm, sem.at[4 + chunks])
    store_g.start()
    both = g_v[...]
    for c in range(chunks):
        part = lax.dot_general(
            saved[:, c * span : (c + 1) * span], both, CONTRACT_FIRST, preferred_element_type=F32
        )
        pg_v[c] = part.astype(BF16).reshape(CHUNK, rows, width)
        copy = pltpu.make_async_copy(
            pg_v.at[c], p_hbm.at[c * CHUNK : (c + 1) * CHUNK, 0:rows, :], sem.at[5 + chunks + c]
        )
        copy.start()
        stores.append(copy)
    store_g.wait()
    for copy in stores:
        copy.wait()


def forward_body(w_ref, r_ref, g_ref, o_ref):
    parts, block, width = w_ref.shape
    half = width // 2
    rows = width // parts
    window = r_ref.shape[0]
    first = w_ref[:, 0:rows, :].reshape(width, width)
    down = w_ref[:, rows:block, :].reshape(half, width)
    fresh = r_ref[:, 0:CAP, :].reshape(-1, width)
    act = dot(fresh, first)
    gate_act = act[:, :half]
    hidden = (gate_act * jax.nn.sigmoid(gate_act) * act[:, half:]).astype(BF16)
    o_ref[:, 0:CAP, :] = dot(hidden, down).astype(BF16).reshape(window, CAP, width)
    grad_input = lax.dot_general(g_ref[...], first, CONTRACT_LAST, preferred_element_type=F32)
    o_ref[:, CAP : 2 * CAP, :] = grad_input.astype(BF16).reshape(window, CAP, width)


def pack(gate, up, down):
    rows, half = gate.shape
    return pl.pallas_call(
        pack_body,
        out_shape=jax.ShapeDtypeStruct((rows + down.shape[0], 2 * half), BF16),
        name="pack_weights",
    )(gate, up, down)


def unpack(summed, rows, low, half, scale):
    return pl.pallas_call(
        functools.partial(unpack_body, scale),
        out_shape=(
            jax.ShapeDtypeStruct((rows, half), F32),
            jax.ShapeDtypeStruct((rows, half), F32),
            jax.ShapeDtypeStruct((low, 2 * half), F32),
        ),
        compiler_params=pltpu.CompilerParams(vmem_limit_bytes=8 * 1024 * 1024),
        name="unpack_grads",
    )(summed)


def land(a, b):
    return pl.pallas_call(
        land_body,
        out_shape=(jax.ShapeDtypeStruct(a.shape, BF16), jax.ShapeDtypeStruct(b.shape, BF16)),
        cost_estimate=pl.CostEstimate(flops=0, bytes_accessed=1 << 20, transcendentals=0),
        name="land",
    )(a, b)


def expert_backward(gathered, received):
    parts, block, width = gathered.shape
    half = width // 2
    rows = width // parts
    chunks = parts // CHUNK
    window = received.shape[0]
    slots = window * CAP
    anywhere = pl.BlockSpec(memory_space=pl.ANY)
    return pl.pallas_call(
        backward_body,
        in_specs=[anywhere, anywhere],
        out_specs=(anywhere, anywhere),
        out_shape=(
            jax.ShapeDtypeStruct(gathered.shape, BF16),
            jax.ShapeDtypeStruct((slots, width), BF16),
        ),
        scratch_shapes=[
            pltpu.VMEM((chunks, CHUNK, rows, width), BF16),
            pltpu.VMEM((parts, block - rows, width), BF16),
            pltpu.VMEM((window, CAP, width), BF16),
            pltpu.VMEM((window, CAP, width), BF16),
            pltpu.VMEM((slots, width), F32),
            pltpu.VMEM((parts, block - rows, width), BF16),
            pltpu.VMEM((chunks, CHUNK, rows, width), BF16),
            pltpu.VMEM((slots, width), BF16),
            pltpu.SemaphoreType.DMA((5 + 2 * chunks,)),
        ],
        compiler_params=pltpu.CompilerParams(vmem_limit_bytes=VMEM_LIMIT),
        cost_estimate=pl.CostEstimate(
            flops=2 * slots * half * width * 6,
            bytes_accessed=8 * 1024 * 1024,
            transcendentals=slots * half,
        ),
        name="expert_backward",
    )(gathered, received)


def expert_forward(gathered, received, grads):
    width = gathered.shape[2]
    window = received.shape[0]
    slots = window * CAP
    return pl.pallas_call(
        forward_body,
        out_shape=jax.ShapeDtypeStruct((window, 2 * CAP, width), BF16),
        compiler_params=pltpu.CompilerParams(vmem_limit_bytes=VMEM_LIMIT),
        cost_estimate=pl.CostEstimate(
            flops=slots * width * width * 5,
            bytes_accessed=6 * 1024 * 1024,
            transcendentals=slots * width // 2,
        ),
        name="expert_forward",
    )(gathered, received, grads)


def local(
    section_input,
    saved_input,
    cotangent,
    routes_forward,
    gates_forward,
    routes_backward,
    gates_backward,
    gate_weight,
    up_weight,
    down_weight,
):
    window = lax.axis_size("expert")
    parts = lax.axis_size("dp")
    token_count = section_input.shape[1]
    model_width = section_input.shape[2]
    half = gate_weight.shape[3]
    rows = gate_weight.shape[2]
    low = down_weight.shape[2]

    own = pack(gate_weight[0, 0], up_weight[0, 0], down_weight[0, 0])
    index = lax.axis_index("dp")
    own = cross_swap(own)
    own, section_input, saved_input, cotangent, routes_forward, routes_backward, gates_backward = (
        lax.optimization_barrier(
            (
                own,
                section_input,
                saved_input,
                cotangent,
                routes_forward,
                routes_backward,
                gates_backward,
            )
        )
    )
    gathered = lax.all_gather(
        own,
        ("dp", "expert"),
        axis=0,
        tiled=True,
        axis_index_groups=cross_rings(),
    ).reshape(parts, rows + low, model_width)

    normed, _ = normalize(section_input[0])
    slot_ids = slot_table(crossed(routes_forward[0], index), window)
    owners = slot_owner(slot_ids, window)
    sent_forward = pad_rows(normed.astype(BF16))[owners].reshape(window, CAP, model_width)
    saved_float, saved_scale = normalize(saved_input[0])
    back_slots = slot_table(crossed(routes_backward[0], index), window)
    back_owners = slot_owner(back_slots, window)
    back_gates = slot_gates(back_slots, gates_backward[0], window)
    sent_backward = pad_rows(saved_float.astype(BF16))[back_owners].reshape(
        window, CAP, model_width
    )
    grad_sent = (back_gates[:, None] * pad_rows(cotangent[0])[back_owners].astype(F32)).astype(BF16)
    grad_sent = grad_sent.reshape(window, CAP, model_width)
    sent = jnp.concatenate([sent_forward, sent_backward, grad_sent], axis=1)
    received = lax.all_to_all(sent, "expert", split_axis=0, concat_axis=0, tiled=True)

    partial, act_grads = expert_backward(gathered, received)
    summed = lax.psum_scatter(
        partial.reshape(parts * (rows + low), model_width),
        ("dp", "expert"),
        scatter_dimension=0,
        axis_index_groups=cross_rings(),
        tiled=True,
    )

    produced = expert_forward(gathered, received, act_grads)
    home = lax.all_to_all(produced, "expert", split_axis=0, concat_axis=0, tiled=True)

    returned_pad = pad_rows(home[:, :CAP].reshape(window * CAP, model_width))
    mixed_sum = section_input[0].astype(F32)
    for slot_pos in range(TOPK):
        mixed_sum = mixed_sum + gates_forward[0][:, slot_pos, None] * returned_pad[
            slot_ids[:, slot_pos]
        ].astype(F32)
    handed = from_behind(mixed_sum.astype(BF16)[None], "section", 1)
    grad_pad = pad_rows(home[:, CAP:].reshape(window * CAP, model_width))
    token_grad = jnp.zeros((token_count, model_width), F32)
    for slot_pos in range(TOPK):
        token_grad = token_grad + grad_pad[back_slots[:, slot_pos]].astype(F32)
    mean_term = jnp.mean(saved_float * token_grad, axis=-1, keepdims=True)
    input_grad = cotangent[0].astype(F32) + saved_scale * (token_grad - saved_float * mean_term)
    grad_back = from_behind(input_grad.astype(BF16)[None], "section", -1)

    handed, grad_back = land(handed, grad_back)
    summed, handed, grad_back = lax.optimization_barrier((summed, handed, grad_back))
    summed = cross_swap(summed)
    grad_scale = 1.0 / math.sqrt(parts * token_count)
    grad_gate, grad_up, grad_down = unpack(summed, rows, low, half, grad_scale)
    return (
        handed,
        grad_back,
        grad_gate[None, None],
        grad_up[None, None],
        grad_down[None, None],
    )


def solution(mesh):
    tokens = P("section", ("dp", "expert"), None)
    weights = P("section", "expert", "dp", None)
    return jax.shard_map(
        local,
        mesh=mesh,
        in_specs=(tokens,) * 7 + (weights,) * 3,
        out_specs=(tokens,) * 2 + (weights,) * 3,
        check_vma=False,
    )
```
